32 devices in a mesh: ctx: 4 (over y, x), rep: 8 (over z, core).
Axes of the slice: x: 2, y: 2, z: 4, core: 2. Of those that a mesh axis runs over, the one named last changes fastest.
Arguments:
- queries: bfloat16 [8, 2048, 8192], P('rep', 'ctx'), may hold values from -20 to 20
- keys: bfloat16 [8, 2048, 1024], P('rep', 'ctx'), may hold values from -20 to 20
- values: bfloat16 [8, 2048, 1024], P('rep', 'ctx'), may hold values from -6 to 6
- doc_lengths: int32 [8, 16], replicated, may hold values from 1 to 512, 2048 in all within a row
Outputs:
- attended: bfloat16 [8, 2048, 8192], P('rep', 'ctx')
The draws below stay inside these ranges and needn't reach their ends.
All inputs are finite; a program needn't handle non-finite values.
Results may differ from the reference program's by a relative error of at most 0.0075.
Values may be sent and summed in bfloat16 or wider, within the bound.
No kernel may reach another device: no remote copies, remote signals or barrier semaphores. Data moves between devices by JAX's collectives and lax.ppermute only.
A program may use at most 192 MiB of HBM per device.

```python
import math
import jax
import jax.numpy as jnp
import numpy as np
from jax import lax

HQ = 64
KEY_HEADS = 8
HEAD_SIZE = 128
S_DEV = 512
NDOC = 16
QUERY_PER_KEY = 8
PACKED_LENGTH = 2048
PACKED_COUNT = 8
N_CTX = 4


def drawn_plan(key):
    common_span = jnp.clip(jax.random.normal(jax.random.fold_in(key, 7), (PACKED_COUNT, PACKED_LENGTH, KEY_HEADS * HEAD_SIZE), jnp.float32), -4.0, 4.0)
    return common_span


def draw_keys(key, part):
    common_span = drawn_plan(key)
    result = common_span
    return result.astype(jnp.bfloat16)


def draw_queries(key, part):
    drawn = jnp.clip(jax.random.normal(jax.random.fold_in(key, 3), (PACKED_COUNT, PACKED_LENGTH, HQ * HEAD_SIZE), jnp.float32), -4.0, 4.0)
    return drawn.astype(jnp.bfloat16)


def shard_levels(stream_key, shape, split, smallest, top_value):
    factor_of = 1.0
    for position, blocks in split:
        heights = jax.random.uniform(jax.random.fold_in(jax.random.fold_in(stream_key, 6), position), (blocks,), jnp.float32, smallest / len(split), top_value / len(split))
        factor_of = factor_of * jnp.repeat(jnp.exp(heights), shape[position] // blocks).reshape((-1,) + (1,) * (len(shape) - 1 - position))
    return factor_of


def profile(number_of, total, limit, skew):
    portions = [(1 << 20) // math.isqrt(standing ** skew) + 1 for standing in range(2, number_of + 1)]
    spare, given = total - limit - (number_of - 1), [1] * (number_of - 1)
    while spare > 0:
        candidates = [i for i in range(number_of - 1) if given[i] < limit]
        pool, remaining = sum([portions[i] for i in candidates]), spare
        for i in candidates:
            extra = min(limit - given[i], max(1, remaining * portions[i] // pool), spare)
            given[i] = given[i] + extra
            spare = spare - extra
    return np.array([limit] + given)


def ragged(rng, number_of, total, reach, skew):
    if number_of == 2:
        one = jax.random.randint(rng, (), max(1, total - reach), min(reach, total - 1) + 1)
        return jnp.stack([one, total - one])
    lengths = jnp.asarray(profile(number_of, total, reach, skew), jnp.int32)
    twos = (number_of - 1) // 2
    donor, receiver = lengths[1:1 + 2 * twos:2], lengths[2:2 + 2 * twos:2]
    slack = jnp.minimum(donor - 1, reach - receiver)
    passed = jax.random.randint(jax.random.fold_in(rng, 1), (twos,), 0, 1 << 20) % (slack + 1)
    lengths = lengths.at[1:1 + 2 * twos:2].set(donor - passed).at[2:2 + 2 * twos:2].set(receiver + passed)
    return lengths[jax.random.permutation(jax.random.fold_in(rng, 2), number_of)]


def bell_draw(key, shape, width, limit, pieces=(), held_as=jnp.bfloat16):
    values = width * jax.random.normal(key, shape, jnp.float32)
    if pieces:
        values = values * shard_levels(key, shape, pieces, -0.22, 0.18)
    return jnp.clip(values, -limit, limit).astype(held_as)


def setup_inputs(seed: int = 0) -> dict:
    splits = jax.random.split(jax.random.key(seed), 5)
    queries = draw_queries(jax.random.fold_in(splits[4], 71), 0)
    keys = draw_keys(jax.random.fold_in(splits[4], 71), 0)
    values = bell_draw(splits[2], (PACKED_COUNT, PACKED_LENGTH, KEY_HEADS * HEAD_SIZE), 1.0, 6.0, ((0, 8), (1, 4)))
    doc_lengths = jax.vmap(lambda own: ragged(own, NDOC, PACKED_LENGTH, PACKED_LENGTH // 4, 2))(jax.random.split(splits[3], PACKED_COUNT)).reshape((PACKED_COUNT, NDOC)).astype(jnp.int32)
    return dict(queries=queries, keys=keys, values=values, doc_lengths=doc_lengths)


def reference(queries, keys, values, doc_lengths):
    doc_ends = jnp.cumsum(doc_lengths, axis=1)
    positions = jnp.arange(PACKED_LENGTH, dtype=jnp.int32)
    segments = jnp.sum((positions[None, :, None] >= doc_ends[:, None, :]).astype(jnp.int32), axis=2)
    scale = HEAD_SIZE ** -0.5
    rows_per_block = S_DEV // 2
    visible_window = rows_per_block + PACKED_LENGTH // 4

    def one_replica(inputs):
        query_rows, rows_of_key, rows_of_value, segment_row = inputs

        def one_block(block):
            start = (block * rows_per_block).astype(jnp.int32)
            key_first_row = jnp.maximum(start + rows_per_block - visible_window, 0).astype(jnp.int32)
            query_tile_rows = lax.dynamic_slice_in_dim(query_rows, start, rows_per_block, 0)
            query_tile_rows = query_tile_rows.reshape(rows_per_block, KEY_HEADS, QUERY_PER_KEY, HEAD_SIZE).astype(jnp.float32)
            heads_of_key = lax.dynamic_slice_in_dim(rows_of_key, key_first_row, visible_window, 0).reshape(visible_window, KEY_HEADS, HEAD_SIZE).astype(jnp.float32)
            heads_of_value = lax.dynamic_slice_in_dim(rows_of_value, key_first_row, visible_window, 0).reshape(visible_window, KEY_HEADS, HEAD_SIZE).astype(jnp.float32)
            query_positions = start + jnp.arange(rows_per_block, dtype=jnp.int32)
            key_positions = key_first_row + jnp.arange(visible_window, dtype=jnp.int32)
            query_segment = lax.dynamic_slice_in_dim(segment_row, start, rows_per_block, 0)
            key_segment = lax.dynamic_slice_in_dim(segment_row, key_first_row, visible_window, 0)
            mask = (key_positions[None, :] <= query_positions[:, None]) & (key_segment[None, :] == query_segment[:, None])
            scores = jnp.einsum("qhgd,khd->hgqk", query_tile_rows, heads_of_key) * scale
            scores = jnp.where(mask[None, None], scores, -1e30)
            top = jnp.max(scores, axis=-1)
            weights = jnp.where(mask[None, None], jnp.exp(scores - top[..., None]), 0.0)
            total = jnp.sum(weights, axis=-1)
            rounded = lax.optimization_barrier(weights.astype(jnp.bfloat16)).astype(jnp.float32)
            output = jnp.einsum("hgqk,khd->hgqd", rounded, heads_of_value) / total[..., None]
            output = jnp.transpose(output, (2, 0, 1, 3)).reshape(rows_per_block, HQ * HEAD_SIZE)
            return output.astype(jnp.bfloat16)

        blocks = lax.map(one_block, jnp.arange(2 * N_CTX, dtype=jnp.int32))
        return blocks.reshape(PACKED_LENGTH, HQ * HEAD_SIZE)

    return lax.map(one_replica, (queries, keys, values, segments))
```

```python
import functools

import jax
import jax.numpy as jnp
from jax import lax
from jax.experimental import pallas as pl
from jax.experimental.pallas import tpu as pltpu
from jax.sharding import PartitionSpec as P

HEAD_SIZE = 128
TILE = 128
GROUPS = 2
PAIR = 8
ONES = 16
NEG = -1e30
LOG2E = 1.4426950408889634
SCALE2 = HEAD_SIZE ** (-0.5) * LOG2E


def first_of(lens_ref, row, base, position):
    start = -base
    first = start
    for d in range(lens_ref.shape[1]):
        first = jnp.where(start <= position, start, first)
        start = start + lens_ref[row, d]
    return first


def end_of(lens_ref, row, base, position):
    end = -base
    found = end
    for d in range(lens_ref.shape[1]):
        found = jnp.where(end <= position, end + lens_ref[row, d], found)
        end = end + lens_ref[row, d]
    return found


def turn_values(value_ref, turned_ref):
    for j in range(value_ref.shape[1] // HEAD_SIZE):
        turned_ref[j, :HEAD_SIZE, :] = value_ref[:, columns_of(j)].T
        turned_ref[j, HEAD_SIZE:, :] = jnp.ones((ONES, value_ref.shape[0]), jnp.bfloat16)


def columns_of(g):
    return slice(g * HEAD_SIZE, (g + 1) * HEAD_SIZE)


def columns_at(unit, i):
    return pl.ds(pl.multiple_of(unit * (PAIR * HEAD_SIZE) + i * HEAD_SIZE, HEAD_SIZE), HEAD_SIZE)


def run_units(units, per_key, q_ref, keys_of, values_of, bias_ref, scratch, finish):
    scores, weights, tops, tops_used = scratch
    rows = bias_ref.shape[0]

    def key_head(unit):
        return lax.div(unit, per_key // PAIR)

    def score(unit):
        unit = jnp.minimum(unit, units - 1)
        q_rows = jnp.concatenate([q_ref[:, columns_at(unit, i)] for i in range(PAIR)], axis=0)
        found = lax.dot_general(
            keys_of(key_head(unit)),
            q_rows,
            (((1,), (1,)), ((), ())),
            preferred_element_type=jnp.float32,
        )
        bias = bias_ref[...]
        found = found + jnp.concatenate([bias] * PAIR, axis=1)
        scores[:rows, :] = found
        tops[...] = jnp.broadcast_to(jnp.max(found, axis=0, keepdims=True) * SCALE2, tops.shape)

    def weigh():
        top = tops[...]
        tops_used[...] = top
        weights[:rows, :] = jnp.exp2(scores[:rows, :] * SCALE2 - top[:1, :]).astype(jnp.bfloat16)

    def close(unit):
        summed = jnp.dot(
            values_of(key_head(unit)), weights[:rows, :], preferred_element_type=jnp.float32
        )
        finish(
            unit, tops_used[:1, :], summed[:HEAD_SIZE], summed[HEAD_SIZE : HEAD_SIZE + 1]
        )

    score(0)
    weigh()
    score(1)

    @pl.loop(0, units)
    def _(unit):
        close(unit)
        weigh()
        score(unit + 2)


def unit_scratch(rows):
    wide = PAIR * TILE
    return [
        pltpu.VMEM((rows, wide), jnp.float32),
        pltpu.VMEM((rows, wide), jnp.bfloat16),
        pltpu.VMEM((8, wide), jnp.float32),
        pltpu.VMEM((8, wide), jnp.float32),
        pltpu.VMEM((rows, TILE), jnp.float32),
    ]


def local_kernel(
    per_key, lens_ref, ids_ref, q_ref, k_ref, v_ref, o_ref, part_ref, lse_ref, plan_ref, turned, *refs
):
    bias_ref = refs[4]
    tile = pl.program_id(0)
    tiles = pl.num_programs(0)
    length = k_ref.shape[0]
    row = ids_ref[0]
    base = ids_ref[1] * length
    units = q_ref.shape[1] // (PAIR * HEAD_SIZE)

    @pl.when(tile == 0)
    def _():
        turn_values(v_ref, turned)
        stop = jnp.clip(end_of(lens_ref, row, base, 0), 0, length)
        straddles = first_of(lens_ref, row, base, 0) < 0
        plan_ref[0] = row
        plan_ref[1] = ids_ref[1]
        plan_ref[2] = jnp.where(straddles, stop, 0)
        plan_ref[3] = jnp.where(straddles, lax.div(stop + TILE - 1, TILE), 1)

    q_at = tile * TILE
    wide = (8, TILE)
    q_pos = q_at + lax.broadcasted_iota(jnp.int32, wide, 1)
    start = -base
    first = jnp.full(wide, start, jnp.int32)
    for d in range(lens_ref.shape[1]):
        first = jnp.where(q_pos >= start, start, first)
        start = start + lens_ref[row, d]

    def finish(unit, top, summed, total):
        result = (summed * (1.0 / total)).astype(o_ref.dtype)
        lse = top + jnp.log2(total)
        for i in range(PAIR):
            own = slice(i * TILE, (i + 1) * TILE)
            at = columns_at(unit, i)
            part_ref[at, :] = result[:, own]
            lse_ref[unit, i : i + 1, :] = lse[:, own]
            o_ref[:, at] = result[:, own].T

    def tile_of(count):
        rows = count * TILE
        k_at = pl.multiple_of((tile + 1 - count) * TILE, TILE)
        for c in range(count):
            k_pos = k_at + c * TILE + lax.broadcasted_iota(jnp.int32, (TILE, TILE), 0)
            seen = (k_pos >= first[:1]) & (k_pos <= q_pos[:1])
            bias_ref[c * TILE : (c + 1) * TILE, :] = jnp.where(seen, 0.0, NEG)

        def keys_of(j):
            return k_ref[
                pl.ds(k_at, rows), pl.ds(pl.multiple_of(j * HEAD_SIZE, HEAD_SIZE), HEAD_SIZE)
            ]

        def values_of(j):
            return turned[j, :, pl.ds(k_at, rows)]

        run_units(
            units,
            per_key,
            q_ref,
            keys_of,
            values_of,
            bias_ref.at[:rows, :],
            refs[:4],
            finish,
        )

    lo = lax.div(jnp.maximum(first_of(lens_ref, row, base, q_at), 0), TILE)
    for n in range(1, length // TILE + 1):

        @pl.when(tile + 1 - lo == n)
        def _(n=n):
            tile_of(n)


def local_attention(queries, keys, values, lens, ids):
    length, width = queries.shape
    per_key = width // keys.shape[1]
    key_heads = keys.shape[1] // HEAD_SIZE
    units = width // (PAIR * HEAD_SIZE)
    return pl.pallas_call(
        functools.partial(local_kernel, per_key),
        out_shape=(
            jax.ShapeDtypeStruct((length, width), queries.dtype),
            jax.ShapeDtypeStruct((width, length), queries.dtype),
            jax.ShapeDtypeStruct((units, 8, length), jnp.float32),
            jax.ShapeDtypeStruct((4,), jnp.int32),
        ),
        grid_spec=pltpu.PrefetchScalarGridSpec(
            num_scalar_prefetch=2,
            grid=(length // TILE,),
            in_specs=[
                pl.BlockSpec((TILE, width), lambda i, *_: (i, 0)),
                pl.BlockSpec(keys.shape, lambda i, *_: (0, 0), pipeline_mode=pl.Buffered(1)),
                pl.BlockSpec(values.shape, lambda i, *_: (0, 0), pipeline_mode=pl.Buffered(1)),
            ],
            out_specs=[
                pl.BlockSpec((TILE, width), lambda i, *_: (i, 0)),
                pl.BlockSpec((width, TILE), lambda i, *_: (0, i)),
                pl.BlockSpec((units, 8, TILE), lambda i, *_: (0, 0, i)),
                pl.BlockSpec(memory_space=pltpu.SMEM),
            ],
            scratch_shapes=[
                pltpu.VMEM((key_heads, HEAD_SIZE + ONES, length), jnp.bfloat16),
                *unit_scratch(length),
            ],
        ),
        cost_estimate=pl.CostEstimate(
            flops=4 * length * length * width,
            bytes_accessed=6 * length * width,
            transcendentals=length * length * width // HEAD_SIZE // 2,
        ),
        compiler_params=pltpu.CompilerParams(vmem_limit_bytes=48 << 20),
        name="local_attention",
    )(lens, ids, queries, keys, values)


def cross_kernel(
    per_key, length, lens_ref, ids_ref, q_ref, part_ref, lse_ref, k_ref, v_ref, _, o_ref, turned, *refs
):
    bias_ref = refs[4]
    tile = pl.program_id(0)
    row = ids_ref[0]
    base = ids_ref[1] * length
    reach = k_ref.shape[0]
    units = q_ref.shape[1] // (PAIR * HEAD_SIZE)
    first = first_of(lens_ref, row, base, 0)
    stop = ids_ref[2]
    key_lo = reach + first
    count = lax.div(reach + TILE - 1 - key_lo, TILE)
    count = jnp.clip(count, 1, reach // TILE)

    @pl.when(tile == 0)
    def _():
        turn_values(v_ref, turned)

    def finish(unit, top, summed, total):
        at = [columns_at(unit, i) for i in range(PAIR)]
        before = jnp.concatenate([lse_ref[unit, i : i + 1, :] for i in range(PAIR)], axis=1)
        old = jnp.concatenate([part_ref[c, :] for c in at], axis=1)
        peak = jnp.maximum(before, top)
        scale_old = jnp.exp2(before - peak)
        scale_new = jnp.exp2(top - peak)
        inverse = 1.0 / (scale_old + scale_new * total)
        result = (scale_old * inverse) * old.astype(jnp.float32) + (
            scale_new * inverse
        ) * summed
        result = result.astype(o_ref.dtype)
        for i in range(PAIR):
            o_ref[:, at[i]] = result[:, i * TILE : (i + 1) * TILE].T

    def tile_of(n):
        rows = n * TILE
        k_at = reach - rows
        k_pos = k_at + lax.broadcasted_iota(jnp.int32, (rows, TILE), 0)
        q_pos = tile * TILE + lax.broadcasted_iota(jnp.int32, (1, TILE), 1)
        bias_ref[:rows, :] = jnp.where((k_pos >= key_lo) & (q_pos < stop), 0.0, NEG)

        def keys_of(j):
            return k_ref[k_at:, pl.ds(pl.multiple_of(j * HEAD_SIZE, HEAD_SIZE), HEAD_SIZE)]

        def values_of(j):
            return turned[j, :, k_at:]

        run_units(
            units,
            per_key,
            q_ref,
            keys_of,
            values_of,
            bias_ref.at[:rows, :],
            refs[:4],
            finish,
        )

    for n in range(1, reach // TILE + 1):

        @pl.when((count == n) & (tile < ids_ref[3]))
        def _(n=n):
            tile_of(n)


def cross_attention(queries, output, part, lse, packed, lens, ids, per_key, group):
    length = queries.shape[0]
    reach, both = packed.shape
    heads = both // 2 // HEAD_SIZE
    wide = heads * per_key * HEAD_SIZE
    units = wide // (PAIR * HEAD_SIZE)

    def at_tile(i, lens, ids):
        return (jnp.minimum(i, ids[3] - 1), group)

    def turned(i, lens, ids):
        return (group, jnp.minimum(i, ids[3] - 1))

    def turned_units(i, lens, ids):
        return (group, 0, jnp.minimum(i, ids[3] - 1))

    def half(which):
        return pl.BlockSpec(
            (reach, both // 2), lambda i, *_: (0, which), pipeline_mode=pl.Buffered(1)
        )

    return pl.pallas_call(
        functools.partial(cross_kernel, per_key, length),
        out_shape=jax.ShapeDtypeStruct(output.shape, output.dtype),
        grid_spec=pltpu.PrefetchScalarGridSpec(
            num_scalar_prefetch=2,
            grid=(length // TILE,),
            in_specs=[
                pl.BlockSpec((TILE, wide), at_tile),
                pl.BlockSpec((wide, TILE), turned),
                pl.BlockSpec((units, 8, TILE), turned_units),
                half(0),
                half(1),
                pl.BlockSpec(memory_space=pl.ANY),
            ],
            out_specs=pl.BlockSpec((TILE, wide), at_tile),
            scratch_shapes=[
                pltpu.VMEM((heads, HEAD_SIZE + ONES, reach), jnp.bfloat16),
                *unit_scratch(reach),
            ],
        ),
        input_output_aliases={7: 0},
        cost_estimate=pl.CostEstimate(
            flops=2 * reach * reach * heads * wide,
            bytes_accessed=4 * reach * heads * wide,
            transcendentals=reach * reach * heads * per_key // 2,
        ),
        compiler_params=pltpu.CompilerParams(vmem_limit_bytes=48 << 20),
        name="cross_attention",
    )(lens, ids, queries, part, lse, packed, packed, output)


def forward(block, hops):
    size = lax.axis_size("ctx")
    return lax.ppermute(block, "ctx", [(i, i + hops) for i in range(size - hops)])


def on_device(queries, keys, values, doc_lengths):
    length = queries.shape[1]
    size = lax.axis_size("ctx")
    blocks_back = min(size - 1, (length * size // 4 - 2 + length) // length)
    per_key = queries.shape[2] // keys.shape[2]
    per_group = keys.shape[2] // GROUPS
    ids = jnp.stack([lax.axis_index("rep"), lax.axis_index("ctx")]).astype(jnp.int32)

    arrived = []
    for g in range(GROUPS):
        columns = slice(g * per_group, (g + 1) * per_group)
        packed = jnp.concatenate([keys[0, :, columns], values[0, :, columns]], axis=1)
        arrived.append([forward(packed, hops) for hops in range(blocks_back, 0, -1)])
    output, part, lse, plan = local_attention(
        queries[0], keys[0], values[0], doc_lengths, ids
    )
    for g in range(GROUPS):
        packed = arrived[g][0] if blocks_back == 1 else jnp.concatenate(arrived[g], axis=0)
        output = cross_attention(
            queries[0], output, part, lse, packed, doc_lengths, plan, per_key, g
        )
    return output[None]


def solution(mesh):
    return jax.shard_map(
        on_device,
        mesh=mesh,
        in_specs=(P("rep", "ctx", None), P("rep", "ctx", None), P("rep", "ctx", None), P()),
        out_specs=P("rep", "ctx", None),
        check_vma=False,
    )
```

```python
import functools

import jax
import jax.numpy as jnp
from jax import lax
from jax.experimental import pallas as pl
from jax.experimental.pallas import tpu as pltpu
from jax.sharding import PartitionSpec as P

HEAD_SIZE = 128
TILE = 128
PAIR = 8
ONES = 16
NEG = -1e30
LOG2E = 1.4426950408889634
SCALE2 = HEAD_SIZE ** (-0.5) * LOG2E


def first_of(lens_ref, row, base, position):
    start = -base
    first = start
    for d in range(lens_ref.shape[1]):
        first = jnp.where(start <= position, start, first)
        start = start + lens_ref[row, d]
    return first


def end_of(lens_ref, row, base, position):
    end = -base
    found = end
    for d in range(lens_ref.shape[1]):
        found = jnp.where(end <= position, end + lens_ref[row, d], found)
        end = end + lens_ref[row, d]
    return found


def turn_values(value_ref, turned_ref):
    for j in range(value_ref.shape[1] // HEAD_SIZE):
        turned_ref[j, :HEAD_SIZE, :] = value_ref[:, columns_of(j)].T
        turned_ref[j, HEAD_SIZE:, :] = jnp.ones((ONES, value_ref.shape[0]), jnp.bfloat16)


def columns_of(g):
    return slice(g * HEAD_SIZE, (g + 1) * HEAD_SIZE)


def columns_at(unit, i, pair=PAIR):
    start = unit * (pair * HEAD_SIZE) + i * HEAD_SIZE
    if isinstance(unit, int):
        return pl.ds(start, HEAD_SIZE)
    return pl.ds(pl.multiple_of(start, HEAD_SIZE), HEAD_SIZE)


def run_units(units, per_key, q_ref, keys_of, values_of, bias_ref, scratch, finish):
    scores, weights, tops, tops_used = scratch
    rows = bias_ref.shape[0]

    def key_head(unit):
        return unit // (per_key // PAIR) if isinstance(unit, int) else lax.div(unit, per_key // PAIR)

    def score(unit):
        q_rows = jnp.concatenate([q_ref[:, columns_at(unit, i)] for i in range(PAIR)], axis=0)
        found = lax.dot_general(
            keys_of(key_head(unit)),
            q_rows,
            (((1,), (1,)), ((), ())),
            preferred_element_type=jnp.float32,
        )
        bias = bias_ref[...]
        found = found + jnp.concatenate([bias] * PAIR, axis=1)
        scores[:rows, :] = found
        tops[...] = jnp.broadcast_to(jnp.max(found, axis=0, keepdims=True) * SCALE2, tops.shape)

    def weigh():
        top = tops[...]
        tops_used[...] = top
        weights[:rows, :] = jnp.exp2(scores[:rows, :] * SCALE2 - top[:1, :]).astype(jnp.bfloat16)

    def close(unit):
        summed = jnp.dot(
            values_of(key_head(unit)), weights[:rows, :], preferred_element_type=jnp.float32
        )
        finish(
            unit, tops_used[:1, :], summed[:HEAD_SIZE], summed[HEAD_SIZE : HEAD_SIZE + 1]
        )

    score(0)
    weigh()
    if units > 1:
        score(1)

        @pl.loop(0, units - 2)
        def _(unit):
            close(unit)
            weigh()
            score(unit + 2)

        close(units - 2)
        weigh()
    close(units - 1)


def unit_scratch(rows):
    wide = PAIR * TILE
    return [
        pltpu.VMEM((rows, wide), jnp.float32),
        pltpu.VMEM((rows, wide), jnp.bfloat16),
        pltpu.VMEM((8, wide), jnp.float32),
        pltpu.VMEM((8, wide), jnp.float32),
        pltpu.VMEM((rows, TILE), jnp.float32),
    ]


def local_kernel(
    per_key, lens_ref, ids_ref, q_ref, k_ref, v_ref, o_ref, part_ref, lse_ref, plan_ref, turned, *refs
):
    bias_ref = refs[4]
    tile = pl.program_id(0)
    tiles = pl.num_programs(0)
    length = k_ref.shape[0]
    row = ids_ref[0]
    base = ids_ref[1] * length
    units = q_ref.shape[1] // (PAIR * HEAD_SIZE)

    @pl.when(tile == 0)
    def _():
        turn_values(v_ref, turned)
        stop = jnp.clip(end_of(lens_ref, row, base, 0), 0, length)
        straddles = first_of(lens_ref, row, base, 0) < 0
        plan_ref[0] = row
        plan_ref[1] = ids_ref[1]
        plan_ref[2] = jnp.where(straddles, stop, 0)
        plan_ref[3] = jnp.where(straddles, lax.div(stop + TILE - 1, TILE), 1)

    q_at = tile * TILE
    wide = (8, TILE)
    q_pos = q_at + lax.broadcasted_iota(jnp.int32, wide, 1)
    start = -base
    first = jnp.full(wide, start, jnp.int32)
    for d in range(lens_ref.shape[1]):
        first = jnp.where(q_pos >= start, start, first)
        start = start + lens_ref[row, d]

    def finish(unit, top, summed, total):
        result = (summed * (1.0 / total)).astype(o_ref.dtype)
        lse = top + jnp.log2(total)
        for i in range(PAIR):
            own = slice(i * TILE, (i + 1) * TILE)
            at = columns_at(unit, i)
            part_ref[at, :] = result[:, own]
            lse_ref[unit, i : i + 1, :] = lse[:, own]
            o_ref[:, at] = result[:, own].T

    def tile_of(count):
        rows = count * TILE
        k_at = pl.multiple_of((tile + 1 - count) * TILE, TILE)
        for c in range(count):
            k_pos = k_at + c * TILE + lax.broadcasted_iota(jnp.int32, (TILE, TILE), 0)
            seen = (k_pos >= first[:1]) & (k_pos <= q_pos[:1])
            bias_ref[c * TILE : (c + 1) * TILE, :] = jnp.where(seen, 0.0, NEG)

        def keys_of(j):
            return k_ref[
                pl.ds(k_at, rows), columns_at(j, 0, 1)
            ]

        def values_of(j):
            return turned[j, :, pl.ds(k_at, rows)]

        run_units(
            units,
            per_key,
            q_ref,
            keys_of,
            values_of,
            bias_ref.at[:rows, :],
            refs[:4],
            finish,
        )

    lo = lax.div(jnp.maximum(first_of(lens_ref, row, base, q_at), 0), TILE)
    for n in range(1, length // TILE + 1):

        @pl.when(tile + 1 - lo == n)
        def _(n=n):
            tile_of(n)


def local_attention(queries, keys, values, lens, ids):
    length, width = queries.shape
    per_key = width // keys.shape[1]
    key_heads = keys.shape[1] // HEAD_SIZE
    units = width // (PAIR * HEAD_SIZE)
    return pl.pallas_call(
        functools.partial(local_kernel, per_key),
        out_shape=(
            jax.ShapeDtypeStruct((length, width), queries.dtype),
            jax.ShapeDtypeStruct((width, length), queries.dtype),
            jax.ShapeDtypeStruct((units, 8, length), jnp.float32),
            jax.ShapeDtypeStruct((4,), jnp.int32),
        ),
        grid_spec=pltpu.PrefetchScalarGridSpec(
            num_scalar_prefetch=2,
            grid=(length // TILE,),
            in_specs=[
                pl.BlockSpec((TILE, width), lambda i, *_: (i, 0)),
                pl.BlockSpec(keys.shape, lambda i, *_: (0, 0), pipeline_mode=pl.Buffered(1)),
                pl.BlockSpec(values.shape, lambda i, *_: (0, 0), pipeline_mode=pl.Buffered(1)),
            ],
            out_specs=[
                pl.BlockSpec((TILE, width), lambda i, *_: (i, 0)),
                pl.BlockSpec((width, TILE), lambda i, *_: (0, i)),
                pl.BlockSpec((units, 8, TILE), lambda i, *_: (0, 0, i)),
                pl.BlockSpec(memory_space=pltpu.SMEM),
            ],
            scratch_shapes=[
                pltpu.VMEM((key_heads, HEAD_SIZE + ONES, length), jnp.bfloat16),
                *unit_scratch(length),
            ],
        ),
        cost_estimate=pl.CostEstimate(
            flops=4 * length * length * width,
            bytes_accessed=6 * length * width,
            transcendentals=length * length * width // HEAD_SIZE // 2,
        ),
        compiler_params=pltpu.CompilerParams(vmem_limit_bytes=48 << 20),
        name="local_attention",
    )(lens, ids, queries, keys, values)


def cross_kernel(
    per_key, length, lens_ref, ids_ref, q_ref, part_ref, lse_ref, k_ref, v_ref, _, o_ref, turned, *refs
):
    bias_ref = refs[4]
    tile = pl.program_id(0)
    row = ids_ref[0]
    base = ids_ref[1] * length
    reach = k_ref.shape[0]
    units = q_ref.shape[1] // (PAIR * HEAD_SIZE)
    first = first_of(lens_ref, row, base, 0)
    stop = ids_ref[2]
    key_lo = reach + first
    count = lax.div(reach + TILE - 1 - key_lo, TILE)
    count = jnp.clip(count, 1, reach // TILE)

    @pl.when(tile == 0)
    def _():
        turn_values(v_ref, turned)

    def finish(unit, top, summed, total):
        at = [columns_at(unit, i) for i in range(PAIR)]
        before = jnp.concatenate([lse_ref[unit, i : i + 1, :] for i in range(PAIR)], axis=1)
        old = jnp.concatenate([part_ref[c, :] for c in at], axis=1)
        peak = jnp.maximum(before, top)
        scale_old = jnp.exp2(before - peak)
        scale_new = jnp.exp2(top - peak)
        inverse = 1.0 / (scale_old + scale_new * total)
        result = (scale_old * inverse) * old.astype(jnp.float32) + (
            scale_new * inverse
        ) * summed
        result = result.astype(o_ref.dtype)
        for i in range(PAIR):
            o_ref[:, at[i]] = result[:, i * TILE : (i + 1) * TILE].T

    def tile_of(n):
        rows = n * TILE
        k_at = reach - rows
        k_pos = k_at + lax.broadcasted_iota(jnp.int32, (rows, TILE), 0)
        q_pos = tile * TILE + lax.broadcasted_iota(jnp.int32, (1, TILE), 1)
        bias_ref[:rows, :] = jnp.where((k_pos >= key_lo) & (q_pos < stop), 0.0, NEG)

        def keys_of(j):
            return k_ref[k_at:, columns_at(j, 0, 1)]

        def values_of(j):
            return turned[j, :, k_at:]

        run_units(
            units,
            per_key,
            q_ref,
            keys_of,
            values_of,
            bias_ref.at[:rows, :],
            refs[:4],
            finish,
        )

    for n in range(1, reach // TILE + 1):

        @pl.when((count == n) & (tile < ids_ref[3]))
        def _(n=n):
            tile_of(n)


def cross_attention(queries, output, part, lse, packed, lens, ids, per_key, at_head):
    length = queries.shape[0]
    reach, both = packed.shape
    heads = both // 2 // HEAD_SIZE
    group = at_head // heads
    wide = heads * per_key * HEAD_SIZE
    units = wide // (PAIR * HEAD_SIZE)

    def at_tile(i, lens, ids):
        return (jnp.minimum(i, ids[3] - 1), group)

    def turned(i, lens, ids):
        return (group, jnp.minimum(i, ids[3] - 1))

    def turned_units(i, lens, ids):
        return (group, 0, jnp.minimum(i, ids[3] - 1))

    def half(which):
        return pl.BlockSpec(
            (reach, both // 2), lambda i, *_: (0, which), pipeline_mode=pl.Buffered(1)
        )

    return pl.pallas_call(
        functools.partial(cross_kernel, per_key, length),
        out_shape=jax.ShapeDtypeStruct(output.shape, output.dtype),
        grid_spec=pltpu.PrefetchScalarGridSpec(
            num_scalar_prefetch=2,
            grid=(length // TILE,),
            in_specs=[
                pl.BlockSpec((TILE, wide), at_tile),
                pl.BlockSpec((wide, TILE), turned),
                pl.BlockSpec((units, 8, TILE), turned_units),
                half(0),
                half(1),
                pl.BlockSpec(memory_space=pl.ANY),
            ],
            out_specs=pl.BlockSpec((TILE, wide), at_tile),
            scratch_shapes=[
                pltpu.VMEM((heads, HEAD_SIZE + ONES, reach), jnp.bfloat16),
                *unit_scratch(reach),
            ],
        ),
        input_output_aliases={7: 0},
        cost_estimate=pl.CostEstimate(
            flops=2 * reach * reach * heads * wide,
            bytes_accessed=4 * reach * heads * wide,
            transcendentals=reach * reach * heads * per_key // 2,
        ),
        compiler_params=pltpu.CompilerParams(vmem_limit_bytes=48 << 20),
        name="cross_attention",
    )(lens, ids, queries, part, lse, packed, packed, output)


def forward(block, hops):
    size = lax.axis_size("ctx")
    return lax.ppermute(block, "ctx", [(i, i + hops) for i in range(size - hops)])


def pack_kernel(k_ref, v_ref, o_ref):
    wide = k_ref.shape[1]
    o_ref[:, :wide] = k_ref[...]
    o_ref[:, wide:] = v_ref[...]


def pack(keys, values, at_head, heads):
    length, wide = keys.shape[0], heads * HEAD_SIZE
    half = pl.BlockSpec((TILE, wide), lambda i: (i, at_head // heads))
    return pl.pallas_call(
        pack_kernel,
        out_shape=jax.ShapeDtypeStruct((length, 2 * wide), keys.dtype),
        grid=(length // TILE,),
        in_specs=[half, half],
        out_specs=pl.BlockSpec((TILE, 2 * wide), lambda i: (i, 0)),
        cost_estimate=pl.CostEstimate(
            flops=0, bytes_accessed=8 * length * wide, transcendentals=0
        ),
        name="pack",
    )(keys, values)


def on_device(queries, keys, values, doc_lengths):
    length = queries.shape[1]
    size = lax.axis_size("ctx")
    blocks_back = min(size - 1, (length * size // 4 - 2 + length) // length)
    per_key = queries.shape[2] // keys.shape[2]
    key_heads = keys.shape[2] // HEAD_SIZE
    last = max(key_heads // 4, 1)
    groups = [(0, key_heads - last), (key_heads - last, last)]
    ids = jnp.stack([lax.axis_index("rep"), lax.axis_index("ctx")]).astype(jnp.int32)

    arrived = []
    for at_head, heads in groups:
        packed = pack(keys[0], values[0], at_head, heads)
        arrived.append([forward(packed, hops) for hops in range(blocks_back, 0, -1)])
    output, part, lse, plan = local_attention(
        queries[0], keys[0], values[0], doc_lengths, ids
    )
    for (at_head, heads), blocks in zip(groups, arrived):
        packed = blocks[0] if blocks_back == 1 else jnp.concatenate(blocks, axis=0)
        output = cross_attention(
            queries[0], output, part, lse, packed, doc_lengths, plan, per_key, at_head
        )
    return output[None]


def solution(mesh):
    return jax.shard_map(
        on_device,
        mesh=mesh,
        in_specs=(P("rep", "ctx", None), P("rep", "ctx", None), P("rep", "ctx", None), P()),
        out_specs=P("rep", "ctx", None),
        check_vma=False,
    )
```

```python
import functools

import jax
import jax.numpy as jnp
from jax import lax
from jax.experimental import pallas as pl
from jax.experimental.pallas import tpu as pltpu
from jax.sharding import PartitionSpec as P

HEAD_SIZE = 128
TILE = 128
PAIR = 8
ONES = 16
NEG = -1e30
LOG2E = 1.4426950408889634
SCALE2 = HEAD_SIZE ** (-0.5) * LOG2E


def first_of(lens_ref, row, base, position):
    start = -base
    first = start
    for d in range(lens_ref.shape[1]):
        first = jnp.where(start <= position, start, first)
        start = start + lens_ref[row, d]
    return first


def end_of(lens_ref, row, base, position):
    end = -base
    found = end
    for d in range(lens_ref.shape[1]):
        found = jnp.where(end <= position, end + lens_ref[row, d], found)
        end = end + lens_ref[row, d]
    return found


def turn_values(value_ref, turned_ref):
    for j in range(value_ref.shape[1] // HEAD_SIZE):
        turned_ref[j, :HEAD_SIZE, :] = value_ref[:, columns_of(j)].T
        turned_ref[j, HEAD_SIZE:, :] = jnp.ones((ONES, value_ref.shape[0]), jnp.bfloat16)


def columns_of(g):
    return slice(g * HEAD_SIZE, (g + 1) * HEAD_SIZE)


def columns_at(unit, i, pair=PAIR):
    start = unit * (pair * HEAD_SIZE) + i * HEAD_SIZE
    if isinstance(unit, int):
        return pl.ds(start, HEAD_SIZE)
    return pl.ds(pl.multiple_of(start, HEAD_SIZE), HEAD_SIZE)


def run_units(units, per_key, q_ref, keys_of, values_of, bias_ref, scratch, finish):
    scores, weights, tops, tops_used = scratch
    rows = bias_ref.shape[0]

    def key_head(unit):
        return unit // (per_key // PAIR) if isinstance(unit, int) else lax.div(unit, per_key // PAIR)

    def score(unit):
        q_rows = jnp.concatenate([q_ref[:, columns_at(unit, i)] for i in range(PAIR)], axis=0)
        found = lax.dot_general(
            keys_of(key_head(unit)),
            q_rows,
            (((1,), (1,)), ((), ())),
            preferred_element_type=jnp.float32,
        )
        bias = bias_ref[...]
        found = found + jnp.concatenate([bias] * PAIR, axis=1)
        scores[:rows, :] = found
        tops[...] = jnp.broadcast_to(jnp.max(found, axis=0, keepdims=True) * SCALE2, tops.shape)

    def weigh():
        top = tops[...]
        tops_used[...] = top
        weights[:rows, :] = jnp.exp2(scores[:rows, :] * SCALE2 - top[:1, :]).astype(jnp.bfloat16)

    def close(unit):
        summed = jnp.dot(
            values_of(key_head(unit)), weights[:rows, :], preferred_element_type=jnp.float32
        )
        finish(
            unit, tops_used[:1, :], summed[:HEAD_SIZE], summed[HEAD_SIZE : HEAD_SIZE + 1]
        )

    score(0)
    weigh()
    if units > 1:
        score(1)

        @pl.loop(0, units - 2)
        def _(unit):
            close(unit)
            weigh()
            score(unit + 2)

        close(units - 2)
        weigh()
    close(units - 1)


def unit_scratch(rows):
    wide = PAIR * TILE
    return [
        pltpu.VMEM((rows, wide), jnp.float32),
        pltpu.VMEM((rows, wide), jnp.bfloat16),
        pltpu.VMEM((8, wide), jnp.float32),
        pltpu.VMEM((8, wide), jnp.float32),
        pltpu.VMEM((rows, TILE), jnp.float32),
    ]


def local_kernel(
    per_key, lens_ref, ids_ref, q_ref, k_ref, v_ref, o_ref, part_ref, lse_ref, plan_ref, turned, *refs
):
    bias_ref = refs[4]
    tile = pl.program_id(0)
    tiles = pl.num_programs(0)
    length = k_ref.shape[0]
    row = ids_ref[0]
    base = ids_ref[1] * length
    units = q_ref.shape[1] // (PAIR * HEAD_SIZE)

    @pl.when(tile == 0)
    def _():
        turn_values(v_ref, turned)
        stop = jnp.clip(end_of(lens_ref, row, base, 0), 0, length)
        straddles = first_of(lens_ref, row, base, 0) < 0
        plan_ref[0] = row
        plan_ref[1] = ids_ref[1]
        plan_ref[2] = jnp.where(straddles, stop, 0)
        plan_ref[3] = jnp.where(straddles, lax.div(stop + TILE - 1, TILE), 1)

    q_at = tile * TILE
    wide = (8, TILE)
    q_pos = q_at + lax.broadcasted_iota(jnp.int32, wide, 1)
    start = -base
    first = jnp.full(wide, start, jnp.int32)
    for d in range(lens_ref.shape[1]):
        first = jnp.where(q_pos >= start, start, first)
        start = start + lens_ref[row, d]

    def finish(unit, top, summed, total):
        result = (summed * (1.0 / total)).astype(o_ref.dtype)
        lse = top + jnp.log2(total)
        for i in range(PAIR):
            own = slice(i * TILE, (i + 1) * TILE)
            at = columns_at(unit, i)
            part_ref[at, :] = result[:, own]
            lse_ref[unit, i : i + 1, :] = lse[:, own]
            o_ref[:, at] = result[:, own].T

    def tile_of(count):
        rows = count * TILE
        k_at = pl.multiple_of((tile + 1 - count) * TILE, TILE)
        for c in range(count):
            k_pos = k_at + c * TILE + lax.broadcasted_iota(jnp.int32, (TILE, TILE), 0)
            seen = (k_pos >= first[:1]) & (k_pos <= q_pos[:1])
            bias_ref[c * TILE : (c + 1) * TILE, :] = jnp.where(seen, 0.0, NEG)

        def keys_of(j):
            return k_ref[
                pl.ds(k_at, rows), columns_at(j, 0, 1)
            ]

        def values_of(j):
            return turned[j, :, pl.ds(k_at, rows)]

        run_units(
            units,
            per_key,
            q_ref,
            keys_of,
            values_of,
            bias_ref.at[:rows, :],
            refs[:4],
            finish,
        )

    lo = lax.div(jnp.maximum(first_of(lens_ref, row, base, q_at), 0), TILE)
    for n in range(1, length // TILE + 1):

        @pl.when(tile + 1 - lo == n)
        def _(n=n):
            tile_of(n)


def local_attention(queries, keys, values, lens, ids):
    length, width = queries.shape
    per_key = width // keys.shape[1]
    key_heads = keys.shape[1] // HEAD_SIZE
    units = width // (PAIR * HEAD_SIZE)
    return pl.pallas_call(
        functools.partial(local_kernel, per_key),
        out_shape=(
            jax.ShapeDtypeStruct((length, width), queries.dtype),
            jax.ShapeDtypeStruct((width, length), queries.dtype),
            jax.ShapeDtypeStruct((units, 8, length), jnp.float32),
            jax.ShapeDtypeStruct((4,), jnp.int32),
        ),
        grid_spec=pltpu.PrefetchScalarGridSpec(
            num_scalar_prefetch=2,
            grid=(length // TILE,),
            in_specs=[
                pl.BlockSpec((TILE, width), lambda i, *_: (i, 0)),
                pl.BlockSpec(keys.shape, lambda i, *_: (0, 0), pipeline_mode=pl.Buffered(1)),
                pl.BlockSpec(values.shape, lambda i, *_: (0, 0), pipeline_mode=pl.Buffered(1)),
            ],
            out_specs=[
                pl.BlockSpec((TILE, width), lambda i, *_: (i, 0)),
                pl.BlockSpec((width, TILE), lambda i, *_: (0, i)),
                pl.BlockSpec((units, 8, TILE), lambda i, *_: (0, 0, i)),
                pl.BlockSpec(memory_space=pltpu.SMEM),
            ],
            scratch_shapes=[
                pltpu.VMEM((key_heads, HEAD_SIZE + ONES, length), jnp.bfloat16),
                *unit_scratch(length),
            ],
        ),
        cost_estimate=pl.CostEstimate(
            flops=4 * length * length * width,
            bytes_accessed=6 * length * width,
            transcendentals=length * length * width // HEAD_SIZE // 2,
        ),
        compiler_params=pltpu.CompilerParams(vmem_limit_bytes=63 << 20),
        name="local_attention",
    )(lens, ids, queries, keys, values)


def cross_kernel(
    per_key, length, lens_ref, ids_ref, q_ref, part_ref, lse_ref, k_ref, v_ref, _, o_ref, turned, *refs
):
    bias_ref = refs[4]
    tile = pl.program_id(0)
    row = ids_ref[0]
    base = ids_ref[1] * length
    reach = k_ref.shape[0]
    units = q_ref.shape[1] // (PAIR * HEAD_SIZE)
    first = first_of(lens_ref, row, base, 0)
    stop = ids_ref[2]
    key_lo = reach + first
    count = lax.div(reach + TILE - 1 - key_lo, TILE)
    count = jnp.clip(count, 1, reach // TILE)

    @pl.when(tile == 0)
    def _():
        turn_values(v_ref, turned)

    def finish(unit, top, summed, total):
        at = [columns_at(unit, i) for i in range(PAIR)]
        before = jnp.concatenate([lse_ref[unit, i : i + 1, :] for i in range(PAIR)], axis=1)
        old = jnp.concatenate([part_ref[c, :] for c in at], axis=1)
        peak = jnp.maximum(before, top)
        scale_old = jnp.exp2(before - peak)
        scale_new = jnp.exp2(top - peak)
        inverse = 1.0 / (scale_old + scale_new * total)
        result = (scale_old * inverse) * old.astype(jnp.float32) + (
            scale_new * inverse
        ) * summed
        result = result.astype(o_ref.dtype)
        for i in range(PAIR):
            o_ref[:, at[i]] = result[:, i * TILE : (i + 1) * TILE].T

    def tile_of(n):
        rows = n * TILE
        k_at = reach - rows
        k_pos = k_at + lax.broadcasted_iota(jnp.int32, (rows, TILE), 0)
        q_pos = tile * TILE + lax.broadcasted_iota(jnp.int32, (1, TILE), 1)
        bias_ref[:rows, :] = jnp.where((k_pos >= key_lo) & (q_pos < stop), 0.0, NEG)

        def keys_of(j):
            return k_ref[k_at:, columns_at(j, 0, 1)]

        def values_of(j):
            return turned[j, :, k_at:]

        run_units(
            units,
            per_key,
            q_ref,
            keys_of,
            values_of,
            bias_ref.at[:rows, :],
            refs[:4],
            finish,
        )

    for n in range(1, reach // TILE + 1):

        @pl.when((count == n) & (tile < ids_ref[3]))
        def _(n=n):
            tile_of(n)


def cross_attention(queries, output, part, lse, packed, lens, ids, per_key, at_head):
    length = queries.shape[0]
    reach, both = packed.shape
    heads = both // 2 // HEAD_SIZE
    group = at_head // heads
    wide = heads * per_key * HEAD_SIZE
    units = wide // (PAIR * HEAD_SIZE)

    def at_tile(i, lens, ids):
        return (jnp.minimum(i, ids[3] - 1), group)

    def turned(i, lens, ids):
        return (group, jnp.minimum(i, ids[3] - 1))

    def turned_units(i, lens, ids):
        return (group, 0, jnp.minimum(i, ids[3] - 1))

    def half(which):
        return pl.BlockSpec(
            (reach, both // 2), lambda i, *_: (0, which), pipeline_mode=pl.Buffered(1)
        )

    return pl.pallas_call(
        functools.partial(cross_kernel, per_key, length),
        out_shape=jax.ShapeDtypeStruct(output.shape, output.dtype),
        grid_spec=pltpu.PrefetchScalarGridSpec(
            num_scalar_prefetch=2,
            grid=(length // TILE,),
            in_specs=[
                pl.BlockSpec((TILE, wide), at_tile),
                pl.BlockSpec((wide, TILE), turned),
                pl.BlockSpec((units, 8, TILE), turned_units),
                half(0),
                half(1),
                pl.BlockSpec(memory_space=pl.ANY),
            ],
            out_specs=pl.BlockSpec((TILE, wide), at_tile),
            scratch_shapes=[
                pltpu.VMEM((heads, HEAD_SIZE + ONES, reach), jnp.bfloat16),
                *unit_scratch(reach),
            ],
        ),
        input_output_aliases={7: 0},
        cost_estimate=pl.CostEstimate(
            flops=2 * reach * reach * heads * wide,
            bytes_accessed=4 * reach * heads * wide,
            transcendentals=reach * reach * heads * per_key // 2,
        ),
        compiler_params=pltpu.CompilerParams(vmem_limit_bytes=48 << 20),
        name="cross_attention",
    )(lens, ids, queries, part, lse, packed, packed, output)


def forward(block, hops):
    size = lax.axis_size("ctx")
    return lax.ppermute(block, "ctx", [(i, i + hops) for i in range(size - hops)])


def pack_kernel(groups, k_ref, v_ref, *refs):
    outs, staged, sems = refs[: len(groups)], refs[len(groups) : -1], refs[-1]
    inward, outward = [], []
    for g, (at_head, heads) in enumerate(groups):
        wide = heads * HEAD_SIZE
        columns = slice(at_head * HEAD_SIZE, at_head * HEAD_SIZE + wide)
        for i, ref in enumerate((k_ref, v_ref)):
            place = staged[g].at[:, i * wide : (i + 1) * wide]
            inward.append(pltpu.make_async_copy(ref.at[:, columns], place, sems.at[3 * g + i]))
        outward.append(pltpu.make_async_copy(staged[g], outs[g], sems.at[3 * g + 2]))
    for copy in inward:
        copy.start()
    for g, copy in enumerate(outward):
        inward[2 * g].wait()
        inward[2 * g + 1].wait()
        copy.start()
    for copy in outward:
        copy.wait()


def pack(keys, values, groups):
    length = keys.shape[0]
    shapes = [(length, 2 * heads * HEAD_SIZE) for _, heads in groups]
    anywhere = pl.BlockSpec(memory_space=pl.ANY)
    return pl.pallas_call(
        functools.partial(pack_kernel, groups),
        out_shape=tuple(jax.ShapeDtypeStruct(shape, keys.dtype) for shape in shapes),
        in_specs=[anywhere, anywhere],
        out_specs=tuple(anywhere for _ in groups),
        scratch_shapes=[
            *(pltpu.VMEM(shape, keys.dtype) for shape in shapes),
            pltpu.SemaphoreType.DMA((3 * len(groups),)),
        ],
        cost_estimate=pl.CostEstimate(
            flops=0, bytes_accessed=8 * length * keys.shape[1], transcendentals=0
        ),
        name="pack",
    )(keys, values)


def on_device(queries, keys, values, doc_lengths):
    length = queries.shape[1]
    size = lax.axis_size("ctx")
    blocks_back = min(size - 1, (length * size // 4 - 2 + length) // length)
    per_key = queries.shape[2] // keys.shape[2]
    key_heads = keys.shape[2] // HEAD_SIZE
    last = max(key_heads // 4, 1)
    groups = [(0, key_heads - last), (key_heads - last, last)]
    ids = jnp.stack([lax.axis_index("rep"), lax.axis_index("ctx")]).astype(jnp.int32)

    arrived = [
        [forward(packed, hops) for hops in range(blocks_back, 0, -1)]
        for packed in pack(keys[0], values[0], groups)
    ]
    output, part, lse, plan = local_attention(
        queries[0], keys[0], values[0], doc_lengths, ids
    )
    for (at_head, heads), blocks in zip(groups, arrived):
        packed = blocks[0] if blocks_back == 1 else jnp.concatenate(blocks, axis=0)
        output = cross_attention(
            queries[0], output, part, lse, packed, doc_lengths, plan, per_key, at_head
        )
    return output[None]


def solution(mesh):
    return jax.shard_map(
        on_device,
        mesh=mesh,
        in_specs=(P("rep", "ctx", None), P("rep", "ctx", None), P("rep", "ctx", None), P()),
        out_specs=P("rep", "ctx", None),
        check_vma=False,
    )
```

```python
import functools

import jax
import jax.numpy as jnp
from jax import lax
from jax.experimental import pallas as pl
from jax.experimental.pallas import tpu as pltpu
from jax.sharding import PartitionSpec as P

HEAD_SIZE = 128
TILE = 128
PAIR = 8
ONES = 16
NEG = -1e30
LOG2E = 1.4426950408889634
SCALE2 = HEAD_SIZE ** (-0.5) * LOG2E


def first_of(lens_ref, row, base, position):
    start = -base
    first = start
    for d in range(lens_ref.shape[1]):
        first = jnp.where(start <= position, start, first)
        start = start + lens_ref[row, d]
    return first


def end_of(lens_ref, row, base, position):
    end = -base
    found = end
    for d in range(lens_ref.shape[1]):
        found = jnp.where(end <= position, end + lens_ref[row, d], found)
        end = end + lens_ref[row, d]
    return found


def turn_values(value_ref, turned_ref):
    for j in range(value_ref.shape[1] // HEAD_SIZE):
        turned_ref[j, :HEAD_SIZE, :] = value_ref[:, columns_of(j)].T
        turned_ref[j, HEAD_SIZE:, :] = jnp.ones((ONES, value_ref.shape[0]), jnp.bfloat16)


def columns_of(g):
    return slice(g * HEAD_SIZE, (g + 1) * HEAD_SIZE)


def columns_at(unit, i, pair=PAIR):
    start = unit * (pair * HEAD_SIZE) + i * HEAD_SIZE
    if isinstance(unit, int):
        return pl.ds(start, HEAD_SIZE)
    return pl.ds(pl.multiple_of(start, HEAD_SIZE), HEAD_SIZE)


def run_units(units, per_key, q_ref, keys_of, values_of, bias_ref, scratch, finish):
    scores, weights, tops, tops_used = scratch
    rows = bias_ref.shape[0]

    def key_head(unit):
        return unit // (per_key // PAIR) if isinstance(unit, int) else lax.div(unit, per_key // PAIR)

    def score(unit):
        q_rows = jnp.concatenate([q_ref[:, columns_at(unit, i)] for i in range(PAIR)], axis=0)
        found = lax.dot_general(
            keys_of(key_head(unit)),
            q_rows,
            (((1,), (1,)), ((), ())),
            preferred_element_type=jnp.float32,
        )
        bias = bias_ref[...]
        found = found + jnp.concatenate([bias] * PAIR, axis=1)
        scores[:rows, :] = found
        tops[...] = jnp.broadcast_to(jnp.max(found, axis=0, keepdims=True) * SCALE2, tops.shape)

    def weigh():
        top = tops[...]
        tops_used[...] = top
        weights[:rows, :] = jnp.exp2(scores[:rows, :] * SCALE2 - top[:1, :]).astype(jnp.bfloat16)

    def close(unit):
        summed = jnp.dot(
            values_of(key_head(unit)), weights[:rows, :], preferred_element_type=jnp.float32
        )
        finish(
            unit, tops_used[:1, :], summed[:HEAD_SIZE], summed[HEAD_SIZE : HEAD_SIZE + 1]
        )

    score(0)
    weigh()
    if units > 1:
        score(1)

        @pl.loop(0, units - 2)
        def _(unit):
            close(unit)
            weigh()
            score(unit + 2)

        close(units - 2)
        weigh()
    close(units - 1)


def unit_scratch(rows):
    wide = PAIR * TILE
    return [
        pltpu.VMEM((rows, wide), jnp.float32),
        pltpu.VMEM((rows, wide), jnp.bfloat16),
        pltpu.VMEM((8, wide), jnp.float32),
        pltpu.VMEM((8, wide), jnp.float32),
        pltpu.VMEM((rows, TILE), jnp.float32),
    ]


def local_kernel(
    per_key, lens_ref, ids_ref, q_ref, k_ref, v_ref, o_ref, part_ref, lse_ref, plan_ref, turned, *refs
):
    bias_ref = refs[4]
    tile = pl.program_id(0)
    tiles = pl.num_programs(0)
    length = k_ref.shape[0]
    row = ids_ref[0]
    base = ids_ref[1] * length
    units = q_ref.shape[1] // (PAIR * HEAD_SIZE)

    @pl.when(tile == 0)
    def _():
        turn_values(v_ref, turned)
        stop = jnp.clip(end_of(lens_ref, row, base, 0), 0, length)
        straddles = first_of(lens_ref, row, base, 0) < 0
        plan_ref[0] = row
        plan_ref[1] = ids_ref[1]
        plan_ref[2] = jnp.where(straddles, stop, 0)
        plan_ref[3] = jnp.where(straddles, lax.div(stop + TILE - 1, TILE), 1)

    q_at = tile * TILE
    wide = (8, TILE)
    q_pos = q_at + lax.broadcasted_iota(jnp.int32, wide, 1)
    start = -base
    first = jnp.full(wide, start, jnp.int32)
    for d in range(lens_ref.shape[1]):
        first = jnp.where(q_pos >= start, start, first)
        start = start + lens_ref[row, d]

    def finish(unit, top, summed, total):
        result = (summed * (1.0 / total)).astype(o_ref.dtype)
        lse = top + jnp.log2(total)
        for i in range(PAIR):
            own = slice(i * TILE, (i + 1) * TILE)
            at = columns_at(unit, i)
            part_ref[at, :] = result[:, own]
            lse_ref[unit, i : i + 1, :] = lse[:, own]
            o_ref[:, at] = result[:, own].T

    def tile_of(count):
        rows = count * TILE
        k_at = pl.multiple_of((tile + 1 - count) * TILE, TILE)
        for c in range(count):
            k_pos = k_at + c * TILE + lax.broadcasted_iota(jnp.int32, (TILE, TILE), 0)
            seen = (k_pos >= first[:1]) & (k_pos <= q_pos[:1])
            bias_ref[c * TILE : (c + 1) * TILE, :] = jnp.where(seen, 0.0, NEG)

        def keys_of(j):
            return k_ref[
                pl.ds(k_at, rows), columns_at(j, 0, 1)
            ]

        def values_of(j):
            return turned[j, :, pl.ds(k_at, rows)]

        run_units(
            units,
            per_key,
            q_ref,
            keys_of,
            values_of,
            bias_ref.at[:rows, :],
            refs[:4],
            finish,
        )

    lo = lax.div(jnp.maximum(first_of(lens_ref, row, base, q_at), 0), TILE)
    for n in range(1, length // TILE + 1):

        @pl.when(tile + 1 - lo == n)
        def _(n=n):
            tile_of(n)


def local_attention(queries, keys, values, lens, ids):
    length, width = queries.shape
    per_key = width // keys.shape[1]
    key_heads = keys.shape[1] // HEAD_SIZE
    units = width // (PAIR * HEAD_SIZE)
    return pl.pallas_call(
        functools.partial(local_kernel, per_key),
        out_shape=(
            jax.ShapeDtypeStruct((length, width), queries.dtype),
            jax.ShapeDtypeStruct((width, length), queries.dtype),
            jax.ShapeDtypeStruct((units, 8, length), jnp.float32),
            jax.ShapeDtypeStruct((4,), jnp.int32),
        ),
        grid_spec=pltpu.PrefetchScalarGridSpec(
            num_scalar_prefetch=2,
            grid=(length // TILE,),
            in_specs=[
                pl.BlockSpec((TILE, width), lambda i, *_: (i, 0)),
                pl.BlockSpec(keys.shape, lambda i, *_: (0, 0), pipeline_mode=pl.Buffered(1)),
                pl.BlockSpec(values.shape, lambda i, *_: (0, 0), pipeline_mode=pl.Buffered(1)),
            ],
            out_specs=[
                pl.BlockSpec((TILE, width), lambda i, *_: (i, 0)),
                pl.BlockSpec((width, TILE), lambda i, *_: (0, i)),
                pl.BlockSpec((units, 8, TILE), lambda i, *_: (0, 0, i)),
                pl.BlockSpec(memory_space=pltpu.SMEM),
            ],
            scratch_shapes=[
                pltpu.VMEM((key_heads, HEAD_SIZE + ONES, length), jnp.bfloat16),
                *unit_scratch(length),
            ],
        ),
        cost_estimate=pl.CostEstimate(
            flops=4 * length * length * width,
            bytes_accessed=6 * length * width,
            transcendentals=length * length * width // HEAD_SIZE // 2,
        ),
        compiler_params=pltpu.CompilerParams(vmem_limit_bytes=63 << 20),
        name="local_attention",
    )(lens, ids, queries, keys, values)


def cross_kernel(
    per_key, length, lens_ref, ids_ref, q_ref, part_ref, lse_ref, k_ref, v_ref, _, o_ref, turned, *refs
):
    bias_ref = refs[4]
    tile = pl.program_id(0)
    row = ids_ref[0]
    base = ids_ref[1] * length
    reach = k_ref.shape[0]
    units = q_ref.shape[1] // (PAIR * HEAD_SIZE)
    first = first_of(lens_ref, row, base, 0)
    stop = ids_ref[2]
    key_lo = reach + first
    wanted = reach - key_lo

    @pl.when(tile == 0)
    def _():
        turn_values(v_ref, turned)

    def finish(unit, top, summed, total):
        at = [columns_at(unit, i) for i in range(PAIR)]
        before = jnp.concatenate([lse_ref[unit, i : i + 1, :] for i in range(PAIR)], axis=1)
        old = jnp.concatenate([part_ref[c, :] for c in at], axis=1)
        peak = jnp.maximum(before, top)
        scale_old = jnp.exp2(before - peak)
        scale_new = jnp.exp2(top - peak)
        inverse = 1.0 / (scale_old + scale_new * total)
        result = (scale_old * inverse) * old.astype(jnp.float32) + (
            scale_new * inverse
        ) * summed
        result = result.astype(o_ref.dtype)
        for i in range(PAIR):
            o_ref[:, at[i]] = result[:, i * TILE : (i + 1) * TILE].T

    def tile_of(rows):
        k_at = reach - rows
        k_pos = k_at + lax.broadcasted_iota(jnp.int32, (rows, TILE), 0)
        q_pos = tile * TILE + lax.broadcasted_iota(jnp.int32, (1, TILE), 1)
        bias_ref[:rows, :] = jnp.where((k_pos >= key_lo) & (q_pos < stop), 0.0, NEG)

        def keys_of(j):
            return k_ref[k_at:, columns_at(j, 0, 1)]

        def values_of(j):
            return turned[j, :, k_at:]

        run_units(
            units,
            per_key,
            q_ref,
            keys_of,
            values_of,
            bias_ref.at[:rows, :],
            refs[:4],
            finish,
        )

    below = -1
    for rows in (32, TILE // 2, *range(TILE, reach + 1, TILE)):

        @pl.when((wanted > below) & (wanted <= rows) & (tile < ids_ref[3]))
        def _(rows=rows):
            tile_of(rows)

        below = rows


def cross_attention(queries, output, part, lse, packed, lens, ids, per_key, at_head):
    length = queries.shape[0]
    reach, both = packed.shape
    heads = both // 2 // HEAD_SIZE
    group = at_head // heads
    wide = heads * per_key * HEAD_SIZE
    units = wide // (PAIR * HEAD_SIZE)

    def at_tile(i, lens, ids):
        return (jnp.minimum(i, ids[3] - 1), group)

    def turned(i, lens, ids):
        return (group, jnp.minimum(i, ids[3] - 1))

    def turned_units(i, lens, ids):
        return (group, 0, jnp.minimum(i, ids[3] - 1))

    def half(which):
        return pl.BlockSpec(
            (reach, both // 2), lambda i, *_: (0, which), pipeline_mode=pl.Buffered(1)
        )

    return pl.pallas_call(
        functools.partial(cross_kernel, per_key, length),
        out_shape=jax.ShapeDtypeStruct(output.shape, output.dtype),
        grid_spec=pltpu.PrefetchScalarGridSpec(
            num_scalar_prefetch=2,
            grid=(length // TILE,),
            in_specs=[
                pl.BlockSpec((TILE, wide), at_tile),
                pl.BlockSpec((wide, TILE), turned),
                pl.BlockSpec((units, 8, TILE), turned_units),
                half(0),
                half(1),
                pl.BlockSpec(memory_space=pl.ANY),
            ],
            out_specs=pl.BlockSpec((TILE, wide), at_tile),
            scratch_shapes=[
                pltpu.VMEM((heads, HEAD_SIZE + ONES, reach), jnp.bfloat16),
                *unit_scratch(reach),
            ],
        ),
        input_output_aliases={7: 0},
        cost_estimate=pl.CostEstimate(
            flops=2 * reach * reach * heads * wide,
            bytes_accessed=4 * reach * heads * wide,
            transcendentals=reach * reach * heads * per_key // 2,
        ),
        compiler_params=pltpu.CompilerParams(vmem_limit_bytes=63 << 20),
        name="cross_attention",
    )(lens, ids, queries, part, lse, packed, packed, output)


def forward(block, hops):
    size = lax.axis_size("ctx")
    return lax.ppermute(block, "ctx", [(i, i + hops) for i in range(size - hops)])


def pack_kernel(groups, k_ref, v_ref, *refs):
    outs, staged, sems = refs[: len(groups)], refs[len(groups) : -1], refs[-1]
    inward, outward = [], []
    for g, (at_head, heads) in enumerate(groups):
        wide = heads * HEAD_SIZE
        columns = slice(at_head * HEAD_SIZE, at_head * HEAD_SIZE + wide)
        for i, ref in enumerate((k_ref, v_ref)):
            place = staged[g].at[:, i * wide : (i + 1) * wide]
            inward.append(pltpu.make_async_copy(ref.at[:, columns], place, sems.at[3 * g + i]))
        outward.append(pltpu.make_async_copy(staged[g], outs[g], sems.at[3 * g + 2]))
    for copy in inward:
        copy.start()
    for g, copy in enumerate(outward):
        inward[2 * g].wait()
        inward[2 * g + 1].wait()
        copy.start()
    for copy in outward:
        copy.wait()


def pack(keys, values, groups):
    length = keys.shape[0]
    shapes = [(length, 2 * heads * HEAD_SIZE) for _, heads in groups]
    anywhere = pl.BlockSpec(memory_space=pl.ANY)
    return pl.pallas_call(
        functools.partial(pack_kernel, groups),
        out_shape=tuple(jax.ShapeDtypeStruct(shape, keys.dtype) for shape in shapes),
        in_specs=[anywhere, anywhere],
        out_specs=tuple(anywhere for _ in groups),
        scratch_shapes=[
            *(pltpu.VMEM(shape, keys.dtype) for shape in shapes),
            pltpu.SemaphoreType.DMA((3 * len(groups),)),
        ],
        cost_estimate=pl.CostEstimate(
            flops=0, bytes_accessed=8 * length * keys.shape[1], transcendentals=0
        ),
        name="pack",
    )(keys, values)


def on_device(queries, keys, values, doc_lengths):
    length = queries.shape[1]
    size = lax.axis_size("ctx")
    blocks_back = min(size - 1, (length * size // 4 - 2 + length) // length)
    per_key = queries.shape[2] // keys.shape[2]
    key_heads = keys.shape[2] // HEAD_SIZE
    last = max(key_heads // 4, 1)
    groups = [(0, key_heads - last), (key_heads - last, last)]
    ids = jnp.stack([lax.axis_index("rep"), lax.axis_index("ctx")]).astype(jnp.int32)

    first, second = pack(keys[0], values[0], groups)
    hops_back = range(blocks_back, 0, -1)
    arrived = [[forward(first, hops) for hops in hops_back]]
    output, part, lse, plan = local_attention(
        queries[0], keys[0], values[0], doc_lengths, ids
    )
    second, plan = lax.optimization_barrier((second, plan))
    arrived.append([forward(second, hops) for hops in hops_back])
    for (at_head, heads), blocks in zip(groups, arrived):
        packed = blocks[0] if blocks_back == 1 else jnp.concatenate(blocks, axis=0)
        output = cross_attention(
            queries[0], output, part, lse, packed, doc_lengths, plan, per_key, at_head
        )
    return output[None]


def solution(mesh):
    return jax.shard_map(
        on_device,
        mesh=mesh,
        in_specs=(P("rep", "ctx", None), P("rep", "ctx", None), P("rep", "ctx", None), P()),
        out_specs=P("rep", "ctx", None),
        check_vma=False,
    )
```

```python
import functools

import jax
import jax.numpy as jnp
from jax import lax
from jax.experimental import pallas as pl
from jax.experimental.pallas import tpu as pltpu
from jax.sharding import PartitionSpec as P


HEAD_SIZE = 128
TILE = 128
PAIR = 8
ONES = 16
NEG = -1e30
LOG2E = 1.4426950408889634
SCALE2 = HEAD_SIZE ** (-0.5) * LOG2E


def first_of(lens_ref, row, base, position):
    start = -base
    first = start
    for d in range(lens_ref.shape[1]):
        first = jnp.where(start <= position, start, first)
        start = start + lens_ref[row, d]
    return first


def end_of(lens_ref, row, base, position):
    end = -base
    found = end
    for d in range(lens_ref.shape[1]):
        found = jnp.where(end <= position, end + lens_ref[row, d], found)
        end = end + lens_ref[row, d]
    return found


def turn_values(value_ref, turned_ref):
    for j in range(value_ref.shape[1] // HEAD_SIZE):
        turned_ref[j, :HEAD_SIZE, :] = value_ref[:, columns_of(j)].T
        turned_ref[j, HEAD_SIZE:, :] = jnp.ones((ONES, value_ref.shape[0]), jnp.bfloat16)


def columns_of(g):
    return slice(g * HEAD_SIZE, (g + 1) * HEAD_SIZE)


def columns_at(unit, i, pair=PAIR):
    start = unit * (pair * HEAD_SIZE) + i * HEAD_SIZE
    if isinstance(unit, int):
        return pl.ds(start, HEAD_SIZE)
    return pl.ds(pl.multiple_of(start, HEAD_SIZE), HEAD_SIZE)


def run_units(units, per_key, q_ref, keys_of, values_of, bias_ref, scratch, finish):
    scores, weights, tops, tops_used = scratch
    rows = bias_ref.shape[0]

    def key_head(unit):
        return unit // (per_key // PAIR) if isinstance(unit, int) else lax.div(unit, per_key // PAIR)

    def score(unit):
        q_rows = jnp.concatenate([q_ref[:, columns_at(unit, i)] for i in range(PAIR)], axis=0)
        found = lax.dot_general(
            keys_of(key_head(unit)),
            q_rows,
            (((1,), (1,)), ((), ())),
            preferred_element_type=jnp.float32,
        )
        bias = bias_ref[...]
        found = found + jnp.concatenate([bias] * PAIR, axis=1)
        scores[:rows, :] = found
        tops[...] = jnp.broadcast_to(jnp.max(found, axis=0, keepdims=True) * SCALE2, tops.shape)

    def weigh():
        top = tops[...]
        tops_used[...] = top
        weights[:rows, :] = jnp.exp2(scores[:rows, :] * SCALE2 - top[:1, :]).astype(jnp.bfloat16)

    def close(unit):
        summed = jnp.dot(
            values_of(key_head(unit)), weights[:rows, :], preferred_element_type=jnp.float32
        )
        finish(
            unit, tops_used[:1, :], summed[:HEAD_SIZE], summed[HEAD_SIZE : HEAD_SIZE + 1]
        )

    score(0)
    weigh()
    if units > 1:
        score(1)

        @pl.loop(0, units - 2)
        def _(unit):
            close(unit)
            weigh()
            score(unit + 2)

        close(units - 2)
        weigh()
    close(units - 1)


def unit_scratch(rows):
    wide = PAIR * TILE
    return [
        pltpu.VMEM((rows, wide), jnp.float32),
        pltpu.VMEM((rows, wide), jnp.bfloat16),
        pltpu.VMEM((8, wide), jnp.float32),
        pltpu.VMEM((8, wide), jnp.float32),
        pltpu.VMEM((rows, TILE), jnp.float32),
    ]


def local_kernel(
    per_key, lens_ref, ids_ref, q_ref, k_ref, v_ref, o_ref, part_ref, lse_ref, plan_ref, turned, *refs
):
    bias_ref = refs[4]
    tile = pl.program_id(0)
    length = k_ref.shape[0]
    row = ids_ref[0]
    base = ids_ref[1] * length
    units = q_ref.shape[1] // (PAIR * HEAD_SIZE)

    @pl.when(tile == 0)
    def _():
        turn_values(v_ref, turned)
        stop = jnp.clip(end_of(lens_ref, row, base, 0), 0, length)
        straddles = first_of(lens_ref, row, base, 0) < 0
        plan_ref[0] = row
        plan_ref[1] = ids_ref[1]
        plan_ref[2] = jnp.where(straddles, stop, 0)
        plan_ref[3] = jnp.where(straddles, lax.div(stop + TILE - 1, TILE), 1)

    q_at = tile * TILE
    wide = (8, TILE)
    q_pos = q_at + lax.broadcasted_iota(jnp.int32, wide, 1)
    start = -base
    first = jnp.full(wide, start, jnp.int32)
    for d in range(lens_ref.shape[1]):
        first = jnp.where(q_pos >= start, start, first)
        start = start + lens_ref[row, d]

    def finish(unit, top, summed, total):
        result = (summed * (1.0 / total)).astype(o_ref.dtype)
        lse = top + jnp.log2(total)
        for i in range(PAIR):
            own = slice(i * TILE, (i + 1) * TILE)
            at = columns_at(unit, i)
            part_ref[at, :] = result[:, own]
            lse_ref[unit, i : i + 1, :] = lse[:, own]
            o_ref[:, at] = result[:, own].T

    def tile_of(count):
        rows = count * TILE
        k_at = pl.multiple_of((tile + 1 - count) * TILE, TILE)
        for c in range(count):
            k_pos = k_at + c * TILE + lax.broadcasted_iota(jnp.int32, (TILE, TILE), 0)
            seen = (k_pos >= first[:1]) & (k_pos <= q_pos[:1])
            bias_ref[c * TILE : (c + 1) * TILE, :] = jnp.where(seen, 0.0, NEG)

        def keys_of(j):
            return k_ref[
                pl.ds(k_at, rows), columns_at(j, 0, 1)
            ]

        def values_of(j):
            return turned[j, :, pl.ds(k_at, rows)]

        run_units(
            units,
            per_key,
            q_ref,
            keys_of,
            values_of,
            bias_ref.at[:rows, :],
            refs[:4],
            finish,
        )

    lo = lax.div(jnp.maximum(first_of(lens_ref, row, base, q_at), 0), TILE)
    for n in range(1, length // TILE + 1):

        @pl.when(tile + 1 - lo == n)
        def _(n=n):
            tile_of(n)


def local_attention(queries, keys, values, lens, ids):
    length, width = queries.shape
    per_key = width // keys.shape[1]
    key_heads = keys.shape[1] // HEAD_SIZE
    units = width // (PAIR * HEAD_SIZE)
    return pl.pallas_call(
        functools.partial(local_kernel, per_key),
        out_shape=(
            jax.ShapeDtypeStruct((length, width), queries.dtype),
            jax.ShapeDtypeStruct((width, length), queries.dtype),
            jax.ShapeDtypeStruct((units, 8, length), jnp.float32),
            jax.ShapeDtypeStruct((4,), jnp.int32),
        ),
        grid_spec=pltpu.PrefetchScalarGridSpec(
            num_scalar_prefetch=2,
            grid=(length // TILE,),
            in_specs=[
                pl.BlockSpec((TILE, width), lambda i, *_: (i, 0)),
                pl.BlockSpec(keys.shape, lambda i, *_: (0, 0), pipeline_mode=pl.Buffered(1)),
                pl.BlockSpec(values.shape, lambda i, *_: (0, 0), pipeline_mode=pl.Buffered(1)),
            ],
            out_specs=[
                pl.BlockSpec((TILE, width), lambda i, *_: (i, 0)),
                pl.BlockSpec((width, TILE), lambda i, *_: (0, i)),
                pl.BlockSpec((units, 8, TILE), lambda i, *_: (0, 0, i)),
                pl.BlockSpec(memory_space=pltpu.SMEM),
            ],
            scratch_shapes=[
                pltpu.VMEM((key_heads, HEAD_SIZE + ONES, length), jnp.bfloat16),
                *unit_scratch(length),
            ],
        ),
        cost_estimate=pl.CostEstimate(
            flops=4 * length * length * width,
            bytes_accessed=6 * length * width,
            transcendentals=length * length * width // HEAD_SIZE // 2,
        ),
        compiler_params=pltpu.CompilerParams(vmem_limit_bytes=63 << 20),
        name="local_attention",
    )(lens, ids, queries, keys, values)


def cross_kernel(
    per_key, length, lens_ref, ids_ref, q_ref, part_ref, lse_ref, k_ref, v_ref, _, o_ref, turned, *refs
):
    bias_ref = refs[4]
    tile = pl.program_id(0)
    row = ids_ref[0]
    base = ids_ref[1] * length
    reach = k_ref.shape[0]
    units = q_ref.shape[1] // (PAIR * HEAD_SIZE)
    first = first_of(lens_ref, row, base, 0)
    stop = ids_ref[2]
    key_lo = reach + first
    wanted = reach - key_lo

    @pl.when(tile == 0)
    def _():
        turn_values(v_ref, turned)

    def finish(unit, top, summed, total):
        at = [columns_at(unit, i) for i in range(PAIR)]
        before = jnp.concatenate([lse_ref[unit, i : i + 1, :] for i in range(PAIR)], axis=1)
        old = jnp.concatenate([part_ref[c, :] for c in at], axis=1)
        peak = jnp.maximum(before, top)
        scale_old = jnp.exp2(before - peak)
        scale_new = jnp.exp2(top - peak)
        inverse = 1.0 / (scale_old + scale_new * total)
        result = (scale_old * inverse) * old.astype(jnp.float32) + (
            scale_new * inverse
        ) * summed
        result = result.astype(o_ref.dtype)
        for i in range(PAIR):
            o_ref[:, at[i]] = result[:, i * TILE : (i + 1) * TILE].T

    def tile_of(rows):
        k_at = reach - rows
        k_pos = k_at + lax.broadcasted_iota(jnp.int32, (rows, TILE), 0)
        q_pos = tile * TILE + lax.broadcasted_iota(jnp.int32, (1, TILE), 1)
        bias_ref[:rows, :] = jnp.where((k_pos >= key_lo) & (q_pos < stop), 0.0, NEG)

        def keys_of(j):
            return k_ref[k_at:, columns_at(j, 0, 1)]

        def values_of(j):
            return turned[j, :, k_at:]

        run_units(
            units,
            per_key,
            q_ref,
            keys_of,
            values_of,
            bias_ref.at[:rows, :],
            refs[:4],
            finish,
        )

    below = -1
    for rows in range(TILE, reach + 1, TILE):

        @pl.when((wanted > below) & (wanted <= rows) & (tile < ids_ref[3]))
        def _(rows=rows):
            tile_of(rows)

        below = rows


def cross_attention(queries, output, part, lse, packed, lens, ids, per_key, at_head, limit):
    length = queries.shape[0]
    reach, both = packed.shape
    heads = both // 2 // HEAD_SIZE
    group = at_head // heads
    wide = heads * per_key * HEAD_SIZE
    units = wide // (PAIR * HEAD_SIZE)

    def at_tile(i, lens, ids):
        return (jnp.minimum(i, ids[3] - 1), group)

    def turned(i, lens, ids):
        return (group, jnp.minimum(i, ids[3] - 1))

    def turned_units(i, lens, ids):
        return (group, 0, jnp.minimum(i, ids[3] - 1))

    def half(which):
        return pl.BlockSpec(
            (reach, both // 2), lambda i, *_: (0, which), pipeline_mode=pl.Buffered(1)
        )

    return pl.pallas_call(
        functools.partial(cross_kernel, per_key, length),
        out_shape=jax.ShapeDtypeStruct(output.shape, output.dtype),
        grid_spec=pltpu.PrefetchScalarGridSpec(
            num_scalar_prefetch=2,
            grid=(length // TILE,),
            in_specs=[
                pl.BlockSpec((TILE, wide), at_tile),
                pl.BlockSpec((wide, TILE), turned),
                pl.BlockSpec((units, 8, TILE), turned_units),
                half(0),
                half(1),
                pl.BlockSpec(memory_space=pl.ANY),
            ],
            out_specs=pl.BlockSpec((TILE, wide), at_tile),
            scratch_shapes=[
                pltpu.VMEM((heads, HEAD_SIZE + ONES, reach), jnp.bfloat16),
                *unit_scratch(reach),
            ],
        ),
        input_output_aliases={7: 0},
        cost_estimate=pl.CostEstimate(
            flops=2 * reach * reach * heads * wide,
            bytes_accessed=4 * reach * heads * wide,
            transcendentals=reach * reach * heads * per_key // 2,
        ),
        compiler_params=pltpu.CompilerParams(vmem_limit_bytes=limit),
        name="cross_attention",
    )(lens, ids, queries, part, lse, packed, packed, output)


def forward(block, hops):
    size = lax.axis_size("ctx")
    return lax.ppermute(block, "ctx", [(i, i + hops) for i in range(size - hops)])


def pack_kernel(groups, k_ref, v_ref, *refs):
    outs, staged, sems = refs[: len(groups)], refs[len(groups) : -1], refs[-1]
    inward, outward = [], []
    for g, (at_head, heads) in enumerate(groups):
        wide = heads * HEAD_SIZE
        columns = slice(at_head * HEAD_SIZE, at_head * HEAD_SIZE + wide)
        for i, ref in enumerate((k_ref, v_ref)):
            place = staged[g].at[:, i * wide : (i + 1) * wide]
            inward.append(pltpu.make_async_copy(ref.at[:, columns], place, sems.at[3 * g + i]))
        outward.append(pltpu.make_async_copy(staged[g], outs[g], sems.at[3 * g + 2]))
    for copy in inward:
        copy.start()
    for g, copy in enumerate(outward):
        inward[2 * g].wait()
        inward[2 * g + 1].wait()
        copy.start()
    for copy in outward:
        copy.wait()


def pack(keys, values, groups):
    length = keys.shape[0]
    shapes = [(length, 2 * heads * HEAD_SIZE) for _, heads in groups]
    anywhere = pl.BlockSpec(memory_space=pl.ANY)
    return pl.pallas_call(
        functools.partial(pack_kernel, groups),
        out_shape=tuple(jax.ShapeDtypeStruct(shape, keys.dtype) for shape in shapes),
        in_specs=[anywhere, anywhere],
        out_specs=tuple(anywhere for _ in groups),
        scratch_shapes=[
            *(pltpu.VMEM(shape, keys.dtype) for shape in shapes),
            pltpu.SemaphoreType.DMA((3 * len(groups),)),
        ],
        cost_estimate=pl.CostEstimate(
            flops=0, bytes_accessed=8 * length * keys.shape[1], transcendentals=0
        ),
        name="pack",
    )(keys, values)


def on_device(queries, keys, values, doc_lengths):
    length = queries.shape[1]
    size = lax.axis_size("ctx")
    blocks_back = min(size - 1, (length * size // 4 - 2 + length) // length)
    per_key = queries.shape[2] // keys.shape[2]
    key_heads = keys.shape[2] // HEAD_SIZE
    shares = [key_heads]
    if key_heads % 4 == 0:
        shares = [key_heads // 2, key_heads // 4, key_heads // 4]
    groups = [(sum(shares[:i]), share) for i, share in enumerate(shares)]
    ids = jnp.stack([lax.axis_index("rep"), lax.axis_index("ctx")]).astype(jnp.int32)

    hops_back = range(blocks_back, 0, -1)
    arrived = []
    for packed in pack(keys[0], values[0], groups):
        arrived.append([forward(packed, hops) for hops in hops_back])
    output, part, lse, plan = local_attention(
        queries[0], keys[0], values[0], doc_lengths, ids
    )
    for (at_head, _), blocks in zip(groups, arrived):
        packed = blocks[0] if blocks_back == 1 else jnp.concatenate(blocks, axis=0)
        output = cross_attention(
            queries[0],
            output,
            part,
            lse,
            packed,
            doc_lengths,
            plan,
            per_key,
            at_head,
            (63 if at_head == 0 else 48) << 20,
        )
    return output[None]


def solution(mesh):
    return jax.shard_map(
        on_device,
        mesh=mesh,
        in_specs=(P("rep", "ctx", None), P("rep", "ctx", None), P("rep", "ctx", None), P()),
        out_specs=P("rep", "ctx", None),
        check_vma=False,
    )
```
